32 devices in a mesh: seq: 8 (over z, x), head: 4 (over y, core).
Axes of the slice: x: 2, y: 2, z: 4, core: 2. Of those that a mesh axis runs over, the one named last changes fastest.
Arguments:
- query_rows: bfloat16 [16384, 1024], P('seq', 'head'), may hold values from -8 to 8
- key_rows: bfloat16 [16384, 1024], P('seq', 'head'), may hold values from -6 to 6
- value_rows: bfloat16 [16384, 1024], P('seq', 'head'), may hold values from -12 to 12
- out_grad: bfloat16 [16384, 1024], P('seq', 'head'), may hold values from -12 to 12
- block_perm: int32 [8, 64], P('head'), may hold values from 0 to 63, as said below
- cut_count: int32 [8], P('head'), may hold values from 1 to 4, as said below
- norm_gain: float32 [1024], P('head'), may hold values from 0.1 to 1.9
Outputs:
- normed_out: bfloat16 [16384, 1024], P('seq', 'head')
- query_grad: bfloat16 [16384, 1024], P('seq', 'head')
- key_grad: bfloat16 [16384, 1024], P('seq', 'head')
- value_grad: bfloat16 [16384, 1024], P('seq', 'head')
- gain_grad: float32 [1024], P('head')
The draws below stay inside these ranges and needn't reach their ends.
Inputs may be any that keep to these rules, and one draw needn't show every extreme that they name: `block_perm`: each row is a permutation of 0 to 63. For every head, of the 8 blocks d * 8 to (d + 1) * 8 - 1, at most 1 are paired with blocks of one range s * 8 to (s + 1) * 8 - 1, and some pair (d, s) reaches 1. `cut_count`: some head has exactly 4.
All inputs are finite; a program needn't handle non-finite values.
Results may differ from the reference program's by a relative error of at most 0.0071.
Values may be sent and summed in bfloat16 or wider, within the bound.
A program may use at most 128 MiB of HBM per device.

```python
import math
import jax
import jax.numpy as jnp
from jax import lax

DH = 128
H = 8
BLOCK = 256
KCUT = 4
BLK_DEV = 8
SEQ = 16384
N_SEQ = 8


def draw_block_perm(key, part):

    def one_head(head_key):
        parts = jax.random.split(head_key, 4)
        alpha = jax.random.permutation(parts[0], N_SEQ)
        beta = jax.random.permutation(parts[1], N_SEQ)
        sigma = jax.random.permutation(parts[2], N_SEQ)
        local_index = jnp.arange(BLK_DEV)
        offset = sigma[local_index % N_SEQ]
        target = jnp.arange(N_SEQ)
        source = alpha[(beta[target][:, None] + offset[None, :]) % N_SEQ]
        shuffles = jax.vmap(lambda row_key: jax.random.permutation(row_key, BLK_DEV))(jax.random.split(parts[3], N_SEQ))
        chosen = shuffles[source, local_index[None, :]]
        return (source * BLK_DEV + chosen).reshape(N_SEQ * BLK_DEV)
    head_keys = jax.random.split(jax.random.fold_in(key, 11), H)
    return jax.vmap(one_head)(head_keys).astype(jnp.int32)


def draw_cut_count(key, part):
    counts = jax.random.randint(jax.random.fold_in(key, 21), (H,), 1, KCUT + 1)
    full_head = jax.random.randint(jax.random.fold_in(key, 22), (), 0, H)
    return jnp.where(jnp.arange(H) == full_head, KCUT, counts).astype(jnp.int32)


def draw_query_rows(key, part):
    row_scale = jnp.exp(jax.random.uniform(jax.random.fold_in(key, 2), (SEQ, 1), minval=math.log(0.3), maxval=math.log(3.0)))
    base = jax.random.normal(jax.random.fold_in(key, 1), (SEQ, H * DH)) * row_scale
    return jnp.clip(base, -8.0, 8.0).astype(jnp.bfloat16)


def draw_key_rows(key, part):
    base = jax.random.normal(jax.random.fold_in(key, 3), (SEQ, H * DH))
    return jnp.clip(base, -6.0, 6.0).astype(jnp.bfloat16)


def draw_value_rows(key, part):
    head_of = (jnp.arange(H * DH) // DH).astype(jnp.float32)
    base = jax.random.normal(jax.random.fold_in(key, 4), (SEQ, H * DH))
    jitter = jnp.exp(jax.random.uniform(jax.random.fold_in(key, 5), (H,), minval=math.log(0.8), maxval=math.log(1.25)))
    head_scale = 3.0 ** (head_of / (H - 1)) * jitter[jnp.arange(H * DH) // DH]
    return jnp.clip(base * head_scale[None, :], -12.0, 12.0).astype(jnp.bfloat16)


def draw_out_grad(key, part):
    place = jnp.arange(SEQ).astype(jnp.float32) / SEQ
    base = jax.random.normal(jax.random.fold_in(key, 6), (SEQ, H * DH))
    token_scale = jnp.exp(jax.random.uniform(jax.random.fold_in(key, 7), (SEQ,), minval=math.log(0.5), maxval=math.log(2.0)))
    base = base * (3.0 ** place * token_scale)[:, None]
    return jnp.clip(base, -12.0, 12.0).astype(jnp.bfloat16)


def setup_inputs(seed: int = 0) -> dict:
    arg_keys = jax.random.split(jax.random.key(seed), 8)
    return {
        "query_rows": draw_query_rows(jax.random.fold_in(arg_keys[7], 71), 0),
        "key_rows": draw_key_rows(jax.random.fold_in(arg_keys[7], 71), 0),
        "value_rows": draw_value_rows(jax.random.fold_in(arg_keys[7], 71), 0),
        "out_grad": draw_out_grad(jax.random.fold_in(arg_keys[7], 71), 0),
        "block_perm": draw_block_perm(jax.random.fold_in(arg_keys[7], 71), 0),
        "cut_count": draw_cut_count(jax.random.fold_in(arg_keys[7], 71), 0),
        "norm_gain": jnp.clip(1.0 + 0.18 * jax.random.normal(arg_keys[6], (H * DH,), jnp.float32), 0.1, 1.9),
    }


def split_heads(rows):
    tokens = rows.shape[0]
    return rows.reshape(tokens // BLOCK, BLOCK, H, DH).transpose(2, 0, 1, 3)

def merge_heads(parts):
    return parts.transpose(1, 2, 0, 3).reshape(parts.shape[1] * parts.shape[2], parts.shape[0] * parts.shape[3])

def attend(query, own_rows, paired_rows, cutoff_rows, live):
    width = query.shape[-1]
    span = own_rows.shape[1]
    count = cutoff_rows.shape[0]
    query_f = query.astype(jnp.float32)
    own = jnp.einsum('gqd,gkd->gqk', query_f, own_rows[..., :width].astype(jnp.float32))
    pair = jnp.einsum('gqd,gkd->gqk', query_f, paired_rows[..., :width].astype(jnp.float32))
    cut = jnp.einsum('gqd,ckd->gqck', query_f, cutoff_rows[..., :width].astype(jnp.float32))
    cut = cut.reshape(query.shape[0], query.shape[1], count * span)
    scores = jnp.concatenate([own, pair, cut], axis=-1) * DH ** (-0.5)
    open_keys = jnp.concatenate([jnp.ones((2 * span,), jnp.bool_), jnp.repeat(live, span)])
    scores = jnp.where(open_keys, scores, -1e+30)
    top = lax.optimization_barrier(jnp.max(scores, axis=-1))
    weights = jnp.exp(scores - top[..., None])
    total = lax.optimization_barrier(jnp.sum(weights, axis=-1))
    return (weights / total[..., None], top, total)

def mix_values(weights, own_rows, paired_rows, cutoff_rows):
    width = own_rows.shape[-1] // 2
    span = own_rows.shape[1]
    count = cutoff_rows.shape[0]
    weights_f = weights.astype(jnp.float32)
    result = jnp.einsum('gqk,gkd->gqd', weights_f[..., :span], own_rows[..., width:].astype(jnp.float32))
    result = result + jnp.einsum('gqk,gkd->gqd', weights_f[..., span:2 * span], paired_rows[..., width:].astype(jnp.float32))
    cut = weights_f[..., 2 * span:].reshape(weights.shape[0], weights.shape[1], count, span)
    return result + jnp.einsum('gqck,ckd->gqd', cut, cutoff_rows[..., width:].astype(jnp.float32))

def head_forward(items):
    query, own_blocks, perm, count = items
    paired = own_blocks[perm]
    cutoff = own_blocks[perm[:KCUT]]
    live = jnp.arange(KCUT) < count
    groups = query.shape[0] // 2

    def step(pieces):
        query_part, own_part, pair_part = pieces
        prob, top, total = attend(query_part, own_part, pair_part, cutoff, live)
        weights = prob.astype(jnp.bfloat16)
        return mix_values(weights, own_part, pair_part, cutoff).astype(jnp.bfloat16)
    result = lax.map(step, (query.reshape(groups, 2, BLOCK, DH), own_blocks.reshape(groups, 2, BLOCK, 2 * DH), paired.reshape(groups, 2, BLOCK, 2 * DH)))
    return result.reshape(query.shape)

def head_backward(items):
    query, own_blocks, perm, count, cotangent = items
    paired = own_blocks[perm]
    cutoff = own_blocks[perm[:KCUT]]
    live = jnp.arange(KCUT) < count
    groups = query.shape[0] // 2
    span = BLOCK

    def step(carry, pieces):
        query_part, own_part, pair_part, cot_part = pieces
        prob, top, total = attend(query_part, own_part, pair_part, cutoff, live)
        weights = prob.astype(jnp.bfloat16).astype(jnp.float32)
        cot_f = cot_part.astype(jnp.float32)
        query_f = query_part.astype(jnp.float32)
        dprob = jnp.concatenate([jnp.einsum('gqd,gkd->gqk', cot_f, own_part[..., DH:].astype(jnp.float32)), jnp.einsum('gqd,gkd->gqk', cot_f, pair_part[..., DH:].astype(jnp.float32)), jnp.einsum('gqd,ckd->gqck', cot_f, cutoff[..., DH:].astype(jnp.float32)).reshape(2, span, KCUT * span)], axis=-1)
        delta = lax.optimization_barrier(jnp.sum(prob * dprob, axis=-1))
        dscore = (prob * (dprob - delta[..., None]) * DH ** (-0.5)).astype(jnp.bfloat16).astype(jnp.float32)
        cut_score = dscore[..., 2 * span:].reshape(2, span, KCUT, span)
        cut_weight = weights[..., 2 * span:].reshape(2, span, KCUT, span)
        query_grad = jnp.einsum('gqk,gkd->gqd', dscore[..., :span], own_part[..., :DH].astype(jnp.float32))
        query_grad = query_grad + jnp.einsum('gqk,gkd->gqd', dscore[..., span:2 * span], pair_part[..., :DH].astype(jnp.float32))
        query_grad = query_grad + jnp.einsum('gqck,ckd->gqd', cut_score, cutoff[..., :DH].astype(jnp.float32))
        own_grad = jnp.concatenate([jnp.einsum('gqk,gqd->gkd', dscore[..., :span], query_f), jnp.einsum('gqk,gqd->gkd', weights[..., :span], cot_f)], axis=-1)
        pair_grad = jnp.concatenate([jnp.einsum('gqk,gqd->gkd', dscore[..., span:2 * span], query_f), jnp.einsum('gqk,gqd->gkd', weights[..., span:2 * span], cot_f)], axis=-1)
        cut_grad = jnp.concatenate([jnp.einsum('gqck,gqd->ckd', cut_score, query_f), jnp.einsum('gqck,gqd->ckd', cut_weight, cot_f)], axis=-1)
        return (carry + cut_grad, (query_grad.astype(jnp.bfloat16), own_grad, pair_grad))
    start = jnp.zeros((KCUT, span, 2 * DH), jnp.float32)
    cut_sum, outputs = lax.scan(step, start, (query.reshape(groups, 2, BLOCK, DH), own_blocks.reshape(groups, 2, BLOCK, 2 * DH), paired.reshape(groups, 2, BLOCK, 2 * DH), cotangent.reshape(groups, 2, BLOCK, DH)))
    query_grad, own_grad, pair_grad = outputs
    own_grad = own_grad.reshape(own_blocks.shape)
    pair_grad = pair_grad.reshape(own_blocks.shape)
    pair_round = lax.optimization_barrier(pair_grad.astype(jnp.bfloat16)).astype(jnp.float32)
    pair_term = jnp.zeros(own_blocks.shape, jnp.float32).at[perm].set(pair_round)
    cut_term = jnp.zeros(own_blocks.shape, jnp.float32).at[perm[:KCUT]].add(cut_sum)
    total_grad = (own_grad + pair_term + cut_term).astype(jnp.bfloat16)
    return (query_grad.reshape(query.shape), total_grad)

def reference(query_rows, key_rows, value_rows, out_grad, block_perm, cut_count, norm_gain):
    query_h = split_heads(query_rows)
    own_blocks = jnp.concatenate([split_heads(key_rows), split_heads(value_rows)], axis=-1)
    attn = lax.map(head_forward, (query_h, own_blocks, block_perm, cut_count))
    attn_f = attn.astype(jnp.float32)
    grad_f = split_heads(out_grad).astype(jnp.float32)
    gain = norm_gain.reshape(H, 1, 1, DH)
    features = H * DH
    square_sum = lax.optimization_barrier(jnp.sum(attn_f * attn_f, axis=(0, 3)))
    mix_sum = lax.optimization_barrier(jnp.sum(gain * grad_f * attn_f, axis=(0, 3)))
    scale_row = lax.rsqrt(square_sum / features + 1e-06)[None, :, :, None]
    normed = (attn_f * scale_row * gain).astype(jnp.bfloat16)
    gain_grad = lax.optimization_barrier(jnp.sum(grad_f * attn_f * scale_row, axis=(1, 2))).reshape(H * DH)
    cotangent = (scale_row * gain * grad_f - attn_f * scale_row ** 3 * mix_sum[None, :, :, None] / features).astype(jnp.bfloat16)
    query_grad, total_grad = lax.map(head_backward, (query_h, own_blocks, block_perm, cut_count, cotangent))
    return (merge_heads(normed), merge_heads(query_grad), merge_heads(total_grad[..., :DH]), merge_heads(total_grad[..., DH:]), gain_grad)
```

```python
import math

import jax
import jax.numpy as jnp
from jax import lax
from jax.experimental import pallas as pl
from jax.experimental.pallas import tpu as pltpu
from jax.sharding import PartitionSpec as P

BLOCK = 256
KCUT = 4
F32 = jnp.float32
BF16 = jnp.bfloat16
NT = (((1,), (1,)), ((), ()))
TN = (((0,), (0,)), ((), ()))
NN = (((1,), (0,)), ((), ()))
VMEM_LIMIT = 48 * 1024 * 1024


def dot(a, b, dims):
    return lax.dot_general(a, b, dims, preferred_element_type=F32)


def params(semantics):
    return pltpu.CompilerParams(
        dimension_semantics=semantics, vmem_limit_bytes=VMEM_LIMIT
    )


def cost(flops, nbytes):
    return pl.CostEstimate(flops=int(flops), bytes_accessed=int(nbytes), transcendentals=0)


def pack_kernel(kv_idx, q_idx, k_ref, v_ref, q_ref, kv_out, q_out):
    width = k_ref.shape[1]
    kv_out[0, 0, :, :width] = k_ref[...]
    kv_out[0, 0, :, width:] = v_ref[...]
    q_out[0, 0] = q_ref[...]


def pack(kv_idx, q_idx, keys, values, query, slots, heads, width):
    spec = pl.BlockSpec((BLOCK, width), lambda s, h, ki, qi: (ki[h, s], h))
    return pl.pallas_call(
        pack_kernel,
        grid_spec=pltpu.PrefetchScalarGridSpec(
            num_scalar_prefetch=2,
            grid=(slots, heads),
            in_specs=[
                spec,
                spec,
                pl.BlockSpec((BLOCK, width), lambda s, h, ki, qi: (qi[h, s], h)),
            ],
            out_specs=[
                pl.BlockSpec((1, 1, BLOCK, 2 * width), lambda s, h, ki, qi: (s, h, 0, 0)),
                pl.BlockSpec((1, 1, BLOCK, width), lambda s, h, ki, qi: (s, h, 0, 0)),
            ],
        ),
        out_shape=[
            jax.ShapeDtypeStruct((slots, heads, BLOCK, 2 * width), BF16),
            jax.ShapeDtypeStruct((slots, heads, BLOCK, width), BF16),
        ],
        compiler_params=params(("arbitrary", "arbitrary")),
        name="pack",
    )(kv_idx, q_idx, keys, values, query)


def cut_kernel(idx, mine, k_ref, v_ref, out):
    width = k_ref.shape[1]
    keep = mine[pl.program_id(0), pl.program_id(1)] > 0
    out[0, 0, :, :width] = jnp.where(keep, k_ref[...], jnp.zeros_like(k_ref))
    out[0, 0, :, width:] = jnp.where(keep, v_ref[...], jnp.zeros_like(v_ref))


def cut_pick(idx, mine, keys, values, heads, width):
    spec = pl.BlockSpec((BLOCK, width), lambda h, c, ci, mi: (ci[h, c], h))
    return pl.pallas_call(
        cut_kernel,
        grid_spec=pltpu.PrefetchScalarGridSpec(
            num_scalar_prefetch=2,
            grid=(heads, KCUT),
            in_specs=[spec, spec],
            out_specs=pl.BlockSpec((1, 1, BLOCK, 2 * width), lambda h, c, ci, mi: (h, c, 0, 0)),
        ),
        out_shape=jax.ShapeDtypeStruct((heads, KCUT, BLOCK, 2 * width), BF16),
        compiler_params=params(("arbitrary", "arbitrary")),
        name="cut_pick",
    )(idx, mine, keys, values)


def forward_kernel(
    slot, count, q_ref, k_ref, v_ref, pair_ref, cut_ref, g_ref, gain_ref, attn_out, stat_out, s_buf
):
    head = pl.program_id(0)
    width = q_ref.shape[1]
    factor = width ** (-0.5) * math.log2(math.e)

    def run(opened):
        query = q_ref[...]
        key_list = [k_ref[...], pair_ref[0, 0, :, :width]]
        value_list = [v_ref[...], pair_ref[0, 0, :, width:]]
        for c in range(opened):
            key_list.append(cut_ref[0, c, :, :width])
            value_list.append(cut_ref[0, c, :, width:])
        top = None
        for j, piece in enumerate(key_list):
            s = dot(piece, query, NT)
            s_buf[j] = s
            high = jnp.max(s, axis=0, keepdims=True)
            top = high if top is None else jnp.maximum(top, high)
        top = top * factor
        total = jnp.zeros_like(top)
        acc = jnp.zeros((width, BLOCK), F32)
        for j, piece in enumerate(value_list):
            e = jnp.exp2(s_buf[j] * factor - top)
            total = total + jnp.sum(e, axis=0, keepdims=True)
            acc = acc + dot(piece, e.astype(BF16), TN)
        attn_t = (acc / total).astype(BF16).astype(F32)
        attn_out[...] = attn_t.T.astype(BF16)
        grad_t = (g_ref[...].astype(F32) * gain_ref[...]).T
        lse = top + jnp.log2(total)
        square = jnp.sum(attn_t * attn_t, axis=0, keepdims=True)
        mix = jnp.sum(grad_t * attn_t, axis=0, keepdims=True)
        stat_out[0, 0] = jnp.concatenate(
            [lse, square, mix, jnp.zeros((5, BLOCK), F32)], axis=0
        )

    for opened in range(1, KCUT + 1):
        pl.when(count[head] == opened)(lambda opened=opened: run(opened))


def forward(slot, count, query, keys, values, pair, cut, grad, gain, heads, width, blocks):
    rows = pl.BlockSpec((BLOCK, width), lambda h, b, s, n: (b, h))
    return pl.pallas_call(
        forward_kernel,
        grid_spec=pltpu.PrefetchScalarGridSpec(
            num_scalar_prefetch=2,
            grid=(heads, blocks),
            in_specs=[
                rows,
                rows,
                rows,
                pl.BlockSpec((1, 1, BLOCK, 2 * width), lambda h, b, s, n: (s[h, b], h, 0, 0)),
                pl.BlockSpec((1, KCUT, BLOCK, 2 * width), lambda h, b, s, n: (h, 0, 0, 0)),
                rows,
                pl.BlockSpec((1, width), lambda h, b, s, n: (0, h)),
            ],
            out_specs=[
                rows,
                pl.BlockSpec((1, 1, 8, BLOCK), lambda h, b, s, n: (h, b, 0, 0)),
            ],
            scratch_shapes=[pltpu.VMEM((2 + KCUT, BLOCK, BLOCK), F32)],
        ),
        out_shape=[
            jax.ShapeDtypeStruct((blocks * BLOCK, heads * width), BF16),
            jax.ShapeDtypeStruct((heads, blocks, 8, BLOCK), F32),
        ],
        compiler_params=params(("arbitrary", "arbitrary")),
        cost_estimate=cost(
            4 * heads * blocks * BLOCK * BLOCK * 6 * width, 10 * blocks * BLOCK * heads * width
        ),
        name="forward",
    )(slot, count, query, keys, values, pair, cut, grad, gain)


def norm_kernel(
    slot, attn_ref, g_ref, gain_ref, stat_ref, row_ref, norm_out, cot_out, send_out, gain_out
):
    width = attn_ref.shape[1]
    attn = attn_ref[...].astype(F32)
    grad = g_ref[...].astype(F32)
    gain = gain_ref[...]
    scale = jnp.broadcast_to(row_ref[0, 0:1, :], (width, BLOCK)).T
    coef = jnp.broadcast_to(row_ref[0, 1:2, :], (width, BLOCK)).T
    scaled = attn * scale
    norm_out[...] = (scaled * gain).astype(BF16)
    cot = (scale * gain * grad - attn * coef).astype(BF16)
    cot_out[0, 0] = cot
    delta = jnp.sum((cot.astype(F32) * attn).T, axis=0, keepdims=True)
    send_out[0, 0] = jnp.concatenate(
        [stat_ref[0, 0, 0:1, :], delta, jnp.zeros((6, BLOCK), F32)], axis=0
    )
    part = jnp.sum((grad * scaled).reshape(BLOCK // 8, 8, width), axis=0)

    @pl.when(pl.program_id(1) == 0)
    def _():
        gain_out[0] = part

    @pl.when(pl.program_id(1) > 0)
    def _():
        gain_out[0] = gain_out[0] + part


def norm(slot, attn, grad, gain, stat, row, heads, width, blocks, slots):
    rows = pl.BlockSpec((BLOCK, width), lambda h, b, s: (b, h))
    return pl.pallas_call(
        norm_kernel,
        grid_spec=pltpu.PrefetchScalarGridSpec(
            num_scalar_prefetch=1,
            grid=(heads, blocks),
            in_specs=[
                rows,
                rows,
                pl.BlockSpec((1, width), lambda h, b, s: (0, h)),
                pl.BlockSpec((1, 1, 8, BLOCK), lambda h, b, s: (h, b, 0, 0)),
                pl.BlockSpec((1, 2, BLOCK), lambda h, b, s: (b, 0, 0)),
            ],
            out_specs=[
                rows,
                pl.BlockSpec((1, 1, BLOCK, width), lambda h, b, s: (s[h, b], h, 0, 0)),
                pl.BlockSpec((1, 1, 8, BLOCK), lambda h, b, s: (s[h, b], h, 0, 0)),
                pl.BlockSpec((1, 8, width), lambda h, b, s: (h, 0, 0)),
            ],
        ),
        out_shape=[
            jax.ShapeDtypeStruct((blocks * BLOCK, heads * width), BF16),
            jax.ShapeDtypeStruct((slots, heads, BLOCK, width), BF16),
            jax.ShapeDtypeStruct((slots, heads, 8, BLOCK), F32),
            jax.ShapeDtypeStruct((heads, 8, width), F32),
        ],
        compiler_params=params(("arbitrary", "arbitrary")),
        name="norm",
    )(slot, attn, grad, gain, stat, row)


def backward_kernel(
    slot, count, q_ref, k_ref, v_ref, pair_ref, cut_ref, cot_ref, stat_ref, dq_out, own_out, cut_out
):
    head = pl.program_id(0)
    width = q_ref.shape[1]
    scale = width ** (-0.5)
    factor = scale * math.log2(math.e)

    @pl.when(pl.program_id(1) == 0)
    def _():
        cut_out[...] = jnp.zeros_like(cut_out)

    def run(opened):
        query = q_ref[...]
        cot = cot_ref[0, 0]
        lse = stat_ref[0, 0, 0:1, :]
        delta = stat_ref[0, 0, 1:2, :]
        key_list = [k_ref[...], pair_ref[0, 0, :, :width]]
        value_list = [v_ref[...], pair_ref[0, 0, :, width:]]
        for c in range(opened):
            key_list.append(cut_ref[0, c, :, :width])
            value_list.append(cut_ref[0, c, :, width:])
        dq = jnp.zeros((width, BLOCK), F32)
        for j in range(2 + opened):
            prob = jnp.exp2(dot(key_list[j], query, NT) * factor - lse)
            dscore = (prob * (dot(value_list[j], cot, NT) - delta)).astype(BF16)
            dq = dq + dot(key_list[j], dscore, TN)
            if j == 1:
                continue
            dk = dot(dscore, query, NN) * scale
            dv = dot(prob.astype(BF16), cot, NN)
            if j == 0:
                own_out[0, 0, :, :width] = dk
                own_out[0, 0, :, width:] = dv
            else:
                cut_out[0, j - 2, :, :width] = cut_out[0, j - 2, :, :width] + dk
                cut_out[0, j - 2, :, width:] = cut_out[0, j - 2, :, width:] + dv
        dq_out[...] = (dq * scale).T.astype(BF16)

    for opened in range(1, KCUT + 1):
        pl.when(count[head] == opened)(lambda opened=opened: run(opened))


def backward(slot, count, query, keys, values, pair, cut, cot, stat, heads, width, blocks):
    rows = pl.BlockSpec((BLOCK, width), lambda h, b, s, n: (b, h))
    return pl.pallas_call(
        backward_kernel,
        grid_spec=pltpu.PrefetchScalarGridSpec(
            num_scalar_prefetch=2,
            grid=(heads, blocks),
            in_specs=[
                rows,
                rows,
                rows,
                pl.BlockSpec((1, 1, BLOCK, 2 * width), lambda h, b, s, n: (s[h, b], h, 0, 0)),
                pl.BlockSpec((1, KCUT, BLOCK, 2 * width), lambda h, b, s, n: (h, 0, 0, 0)),
                pl.BlockSpec((1, 1, BLOCK, width), lambda h, b, s, n: (s[h, b], h, 0, 0)),
                pl.BlockSpec((1, 1, 8, BLOCK), lambda h, b, s, n: (s[h, b], h, 0, 0)),
            ],
            out_specs=[
                rows,
                pl.BlockSpec((1, 1, BLOCK, 2 * width), lambda h, b, s, n: (h, b, 0, 0)),
                pl.BlockSpec((1, KCUT, BLOCK, 2 * width), lambda h, b, s, n: (h, 0, 0, 0)),
            ],
        ),
        out_shape=[
            jax.ShapeDtypeStruct((blocks * BLOCK, heads * width), BF16),
            jax.ShapeDtypeStruct((heads, blocks, BLOCK, 2 * width), F32),
            jax.ShapeDtypeStruct((heads, KCUT, BLOCK, 2 * width), F32),
        ],
        compiler_params=params(("arbitrary", "arbitrary")),
        cost_estimate=cost(
            10 * heads * blocks * BLOCK * BLOCK * 6 * width, 12 * blocks * BLOCK * heads * width
        ),
        name="backward",
    )(slot, count, query, keys, values, pair, cut, cot, stat)


def owner_kernel(
    slot, which, k_ref, v_ref, q_ref, cot_ref, stat_ref, own_ref, cut_ref, dk_out, dv_out
):
    width = k_ref.shape[1]
    scale = width ** (-0.5)
    factor = scale * math.log2(math.e)
    query = q_ref[0, 0]
    cot = cot_ref[0, 0]
    prob = jnp.exp2(dot(k_ref[...], query, NT) * factor - stat_ref[0, 0, 0:1, :])
    dscore = (prob * (dot(v_ref[...], cot, NT) - stat_ref[0, 0, 1:2, :])).astype(BF16)
    dk = (dot(dscore, query, NN) * scale).astype(BF16).astype(F32)
    dv = dot(prob.astype(BF16), cot, NN).astype(BF16).astype(F32)
    dk = dk + own_ref[0, 0, :, :width]
    dv = dv + own_ref[0, 0, :, width:]
    c = which[pl.program_id(0), pl.program_id(1)]

    @pl.when(c < 0)
    def _():
        dk_out[...] = dk.astype(BF16)
        dv_out[...] = dv.astype(BF16)

    @pl.when(c >= 0)
    def _():
        place = jnp.maximum(c, 0)
        dk_out[...] = (dk + cut_ref[0, place, :, :width].astype(F32)).astype(BF16)
        dv_out[...] = (dv + cut_ref[0, place, :, width:].astype(F32)).astype(BF16)


def owner(slot, which, keys, values, query, cot, stat, own, cut, heads, width, blocks):
    rows = pl.BlockSpec((BLOCK, width), lambda h, b, s, w: (b, h))
    return pl.pallas_call(
        owner_kernel,
        grid_spec=pltpu.PrefetchScalarGridSpec(
            num_scalar_prefetch=2,
            grid=(heads, blocks),
            in_specs=[
                rows,
                rows,
                pl.BlockSpec((1, 1, BLOCK, width), lambda h, b, s, w: (s[h, b], h, 0, 0)),
                pl.BlockSpec((1, 1, BLOCK, width), lambda h, b, s, w: (s[h, b], h, 0, 0)),
                pl.BlockSpec((1, 1, 8, BLOCK), lambda h, b, s, w: (s[h, b], h, 0, 0)),
                pl.BlockSpec((1, 1, BLOCK, 2 * width), lambda h, b, s, w: (h, b, 0, 0)),
                pl.BlockSpec((1, KCUT, BLOCK, 2 * width), lambda h, b, s, w: (h, 0, 0, 0)),
            ],
            out_specs=[rows, rows],
        ),
        out_shape=[jax.ShapeDtypeStruct((blocks * BLOCK, heads * width), BF16)] * 2,
        compiler_params=params(("arbitrary", "arbitrary")),
        name="owner",
    )(slot, which, keys, values, query, cot, stat, own, cut)


def exchange(x):
    return lax.all_to_all(x, "seq", split_axis=0, concat_axis=0, tiled=True)


def body(query_rows, key_rows, value_rows, out_grad, block_perm, cut_count, norm_gain):
    heads = block_perm.shape[0]
    width = query_rows.shape[1] // heads
    blocks = query_rows.shape[0] // BLOCK
    slots = lax.axis_size("seq")
    features = lax.axis_size("head") * heads * width
    position = lax.axis_index("seq")
    by_dev = block_perm.reshape(heads, slots, blocks)
    local_perm = lax.dynamic_index_in_dim(by_dev, position, 1, keepdims=False)
    recv_slot = local_perm // blocks
    kv_idx = jnp.sum(jnp.where(by_dev // blocks == position, by_dev % blocks, 0), axis=2)
    place = jnp.arange(blocks)
    q_idx = jnp.sum(
        jnp.where(
            recv_slot[:, None, :] == jnp.arange(slots)[None, :, None], place[None, None, :], 0
        ),
        axis=2,
    )
    owned = position * blocks + place
    hits = block_perm[:, None, :] == owned[None, :, None]
    send_slot = jnp.sum(
        jnp.where(hits, (jnp.arange(slots * blocks) // blocks)[None, None, :], 0), axis=2
    )
    cut_global = block_perm[:, :KCUT]
    cut_mine = (cut_global // blocks == position).astype(jnp.int32)
    cut_local = cut_global % blocks
    is_cut = (cut_mine[:, :, None] > 0) & (cut_local[:, :, None] == place[None, None, :])
    which = jnp.sum(jnp.where(is_cut, jnp.arange(1, KCUT + 1)[None, :, None], 0), axis=1) - 1
    gain = norm_gain.reshape(1, heads * width)

    cut_rows = lax.psum(
        cut_pick(cut_local, cut_mine, key_rows, value_rows, heads, width), "seq"
    )
    kv_send, q_send = pack(kv_idx, q_idx, key_rows, value_rows, query_rows, slots, heads, width)
    kv_recv = exchange(kv_send)
    q_recv = exchange(q_send)
    attn, stat = forward(
        recv_slot, cut_count, query_rows, key_rows, value_rows, kv_recv, cut_rows,
        out_grad, gain, heads, width, blocks,
    )
    sums = lax.psum(jnp.sum(stat[:, :, 1:3, :], axis=0), "head")
    scale_row = lax.rsqrt(sums[:, 0] / features + 1e-06)
    coef = scale_row**3 * sums[:, 1] / features
    row = jnp.stack([scale_row, coef], axis=1)
    normed, cot_send, stat_send, gain_part = norm(
        recv_slot, attn, out_grad, gain, stat, row, heads, width, blocks, slots
    )
    cot_recv = exchange(cot_send)
    stat_recv = exchange(stat_send)
    query_grad, own_grad, cut_grad = backward(
        recv_slot, cut_count, query_rows, key_rows, value_rows, kv_recv, cut_rows,
        cot_send, stat_send, heads, width, blocks,
    )
    gain_total = lax.psum(jnp.sum(gain_part, axis=1), "seq")
    cut_total = lax.psum(cut_grad.astype(BF16), "seq")
    key_grad, value_grad = owner(
        send_slot, which, key_rows, value_rows, q_recv, cot_recv, stat_recv, own_grad,
        cut_total, heads, width, blocks,
    )
    return normed, query_grad, key_grad, value_grad, gain_total.reshape(heads * width)


def solution(mesh):
    rows = P("seq", "head")
    return jax.shard_map(
        body,
        mesh=mesh,
        in_specs=(rows, rows, rows, rows, P("head", None), P("head"), P("head")),
        out_specs=(rows, rows, rows, rows, P("head")),
        check_vma=False,
    )
```

```python
import math

import jax
import jax.numpy as jnp
from jax import lax
from jax.experimental import pallas as pl
from jax.experimental.pallas import tpu as pltpu
from jax.sharding import PartitionSpec as P

BLOCK = 256
KCUT = 4
F32 = jnp.float32
BF16 = jnp.bfloat16
NT = (((1,), (1,)), ((), ()))
TN = (((0,), (0,)), ((), ()))
NN = (((1,), (0,)), ((), ()))
VMEM_LIMIT = 48 * 1024 * 1024


def dot(a, b, dims):
    return lax.dot_general(a, b, dims, preferred_element_type=F32)


def params(semantics):
    return pltpu.CompilerParams(
        dimension_semantics=semantics, vmem_limit_bytes=VMEM_LIMIT
    )


def cost(flops, nbytes):
    return pl.CostEstimate(flops=int(flops), bytes_accessed=int(nbytes), transcendentals=0)


EXTRA = 16


def split3(x):
    first = x.astype(BF16)
    rest = x - first.astype(F32)
    second = rest.astype(BF16)
    third = (rest - second.astype(F32)).astype(BF16)
    return [first.astype(F32), second.astype(F32), third.astype(F32)]


def write_stats(ref, values, width):
    pieces = []
    for value in values:
        for piece in split3(value):
            for start in range(0, BLOCK, width):
                pieces.append(piece[:, start : start + width])
    pieces.append(jnp.zeros((EXTRA - len(pieces), width), F32))
    ref[0, 0, BLOCK:, :] = jnp.concatenate(pieces, axis=0).astype(BF16)


def read_stats(ref, width):
    rows = ref[0, 0, BLOCK:, :].astype(F32)
    halves = BLOCK // width
    values = []
    for v in range(2):
        parts = []
        for h in range(halves):
            base = v * 3 * halves + h
            low = rows[base + 2 * halves : base + 2 * halves + 1]
            mid = rows[base + halves : base + halves + 1]
            parts.append(rows[base : base + 1] + (mid + low))
        values.append(jnp.concatenate(parts, axis=1))
    return values


def pack_kernel(kv_idx, q_idx, c_idx, k_ref, v_ref, q_ref, kc_ref, vc_ref, kv_out, q_out, cut_out):
    width = k_ref.shape[1]
    kv_out[0, 0, :, :width] = k_ref[...]
    kv_out[0, 0, :, width:] = v_ref[...]
    q_out[0, 0] = q_ref[...]

    @pl.when(pl.program_id(1) == 0)
    def _():
        cut_out[0, 0, :, :width] = kc_ref[...]
        cut_out[0, 0, :, width:] = vc_ref[...]


def pack(kv_idx, q_idx, c_idx, keys, values, query, slots, heads, width):
    own = pl.BlockSpec((BLOCK, width), lambda h, s, ki, qi, ci: (ki[h, s], h))
    cut = pl.BlockSpec((BLOCK, width), lambda h, s, ki, qi, ci: (ci[h], h))
    return pl.pallas_call(
        pack_kernel,
        grid_spec=pltpu.PrefetchScalarGridSpec(
            num_scalar_prefetch=3,
            grid=(heads, slots),
            in_specs=[
                own,
                own,
                pl.BlockSpec((BLOCK, width), lambda h, s, ki, qi, ci: (qi[h, s], h)),
                cut,
                cut,
            ],
            out_specs=[
                pl.BlockSpec((1, 1, BLOCK, 2 * width), lambda h, s, ki, qi, ci: (s, h, 0, 0)),
                pl.BlockSpec((1, 1, BLOCK, width), lambda h, s, ki, qi, ci: (s, h, 0, 0)),
                pl.BlockSpec((1, 1, BLOCK, 2 * width), lambda h, s, ki, qi, ci: (0, h, 0, 0)),
            ],
        ),
        out_shape=[
            jax.ShapeDtypeStruct((slots, heads, BLOCK, 2 * width), BF16),
            jax.ShapeDtypeStruct((slots, heads, BLOCK, width), BF16),
            jax.ShapeDtypeStruct((1, heads, BLOCK, 2 * width), BF16),
        ],
        compiler_params=params(("arbitrary", "arbitrary")),
        name="pack",
    )(kv_idx, q_idx, c_idx, keys, values, query, keys, values)


def forward_kernel(
    slot, count, dev, q_ref, k_ref, v_ref, pair_ref, cut_ref, g_ref, gain_ref, attn_out, stat_out, s_buf
):
    head = pl.program_id(0)
    width = q_ref.shape[1]
    factor = width ** (-0.5) * math.log2(math.e)

    def run(opened):
        query = q_ref[...]
        key_list = [k_ref[...], pair_ref[0, 0, :, :width]]
        value_list = [v_ref[...], pair_ref[0, 0, :, width:]]
        for c in range(opened):
            key_list.append(cut_ref[dev[head, c], 0, :, :width])
            value_list.append(cut_ref[dev[head, c], 0, :, width:])
        top = None
        for j, piece in enumerate(key_list):
            s = dot(piece, query, NT)
            s_buf[j] = s
            high = jnp.max(s, axis=0, keepdims=True)
            top = high if top is None else jnp.maximum(top, high)
        top = top * factor
        total = jnp.zeros_like(top)
        acc = jnp.zeros((width, BLOCK), F32)
        for j, piece in enumerate(value_list):
            e = jnp.exp2(s_buf[j] * factor - top)
            total = total + jnp.sum(e, axis=0, keepdims=True)
            acc = acc + dot(piece, e.astype(BF16), TN)
        attn_t = (acc / total).astype(BF16).astype(F32)
        attn_out[...] = attn_t.T.astype(BF16)
        grad_t = (g_ref[...].astype(F32) * gain_ref[...]).T
        lse = top + jnp.log2(total)
        square = jnp.sum(attn_t * attn_t, axis=0, keepdims=True)
        mix = jnp.sum(grad_t * attn_t, axis=0, keepdims=True)
        stat_out[0, 0] = jnp.concatenate(
            [lse, square, mix, jnp.zeros((5, BLOCK), F32)], axis=0
        )

    for opened in range(1, KCUT + 1):
        pl.when(count[head] == opened)(lambda opened=opened: run(opened))


def forward(slot, count, dev, query, keys, values, pair, cut, grad, gain, heads, width, blocks):
    rows = pl.BlockSpec((BLOCK, width), lambda h, b, s, n, d: (b, h))
    return pl.pallas_call(
        forward_kernel,
        grid_spec=pltpu.PrefetchScalarGridSpec(
            num_scalar_prefetch=3,
            grid=(heads, blocks),
            in_specs=[
                rows,
                rows,
                rows,
                pl.BlockSpec((1, 1, BLOCK, 2 * width), lambda h, b, s, n, d: (s[h, b], h, 0, 0)),
                pl.BlockSpec((cut.shape[0], 1, BLOCK, 2 * width), lambda h, b, s, n, d: (0, h, 0, 0)),
                rows,
                pl.BlockSpec((1, width), lambda h, b, s, n, d: (0, h)),
            ],
            out_specs=[
                rows,
                pl.BlockSpec((1, 1, 8, BLOCK), lambda h, b, s, n, d: (h, b, 0, 0)),
            ],
            scratch_shapes=[pltpu.VMEM((2 + KCUT, BLOCK, BLOCK), F32)],
        ),
        out_shape=[
            jax.ShapeDtypeStruct((blocks * BLOCK, heads * width), BF16),
            jax.ShapeDtypeStruct((heads, blocks, 8, BLOCK), F32),
        ],
        compiler_params=params(("arbitrary", "arbitrary")),
        cost_estimate=cost(
            4 * heads * blocks * BLOCK * BLOCK * 6 * width, 10 * blocks * BLOCK * heads * width
        ),
        name="forward",
    )(slot, count, dev, query, keys, values, pair, cut, grad, gain)


def norm_kernel(
    slot, attn_ref, g_ref, gain_ref, stat_ref, row_ref, norm_out, cot_out, gain_out, gain_buf
):
    width = attn_ref.shape[1]
    attn = attn_ref[...].astype(F32)
    grad = g_ref[...].astype(F32)
    gain = gain_ref[...]
    scale = jnp.broadcast_to(row_ref[0, 0:1, :], (width, BLOCK)).T
    coef = jnp.broadcast_to(row_ref[0, 1:2, :], (width, BLOCK)).T
    scaled = attn * scale
    norm_out[...] = (scaled * gain).astype(BF16)
    cot = (scale * gain * grad - attn * coef).astype(BF16)
    cot_out[0, 0, :BLOCK, :] = cot
    delta = jnp.sum((cot.astype(F32) * attn).T, axis=0, keepdims=True)
    write_stats(cot_out, [stat_ref[0, 0, 0:1, :], delta], width)
    part = jnp.sum((grad * scaled).reshape(BLOCK // 8, 8, width), axis=0)

    @pl.when(pl.program_id(1) == 0)
    def _():
        gain_buf[...] = part

    @pl.when(pl.program_id(1) > 0)
    def _():
        gain_buf[...] = gain_buf[...] + part

    @pl.when(pl.program_id(1) == pl.num_programs(1) - 1)
    def _():
        pieces = split3(jnp.sum(gain_buf[...], axis=0, keepdims=True))
        pieces.append(jnp.zeros((EXTRA - 3, width), F32))
        gain_out[0] = jnp.concatenate(pieces, axis=0).astype(BF16)


def norm(slot, attn, grad, gain, stat, row, heads, width, blocks, slots):
    rows = pl.BlockSpec((BLOCK, width), lambda h, b, s: (b, h))
    return pl.pallas_call(
        norm_kernel,
        grid_spec=pltpu.PrefetchScalarGridSpec(
            num_scalar_prefetch=1,
            grid=(heads, blocks),
            in_specs=[
                rows,
                rows,
                pl.BlockSpec((1, width), lambda h, b, s: (0, h)),
                pl.BlockSpec((1, 1, 8, BLOCK), lambda h, b, s: (h, b, 0, 0)),
                pl.BlockSpec((1, 2, BLOCK), lambda h, b, s: (b, 0, 0)),
            ],
            out_specs=[
                rows,
                pl.BlockSpec((1, 1, BLOCK + EXTRA, width), lambda h, b, s: (s[h, b], h, 0, 0)),
                pl.BlockSpec((1, EXTRA, width), lambda h, b, s: (h, 0, 0)),
            ],
            scratch_shapes=[pltpu.VMEM((8, width), F32)],
        ),
        out_shape=[
            jax.ShapeDtypeStruct((blocks * BLOCK, heads * width), BF16),
            jax.ShapeDtypeStruct((slots, heads, BLOCK + EXTRA, width), BF16),
            jax.ShapeDtypeStruct((heads, EXTRA, width), BF16),
        ],
        compiler_params=params(("arbitrary", "arbitrary")),
        name="norm",
    )(slot, attn, grad, gain, stat, row)


def cut_kernel(slot, count, dev, q_ref, cut_ref, cot_ref, dq_out, cut_out, sums):
    head = pl.program_id(0)
    step = pl.program_id(1)
    width = q_ref.shape[1]
    scale = width ** (-0.5)
    factor = scale * math.log2(math.e)

    @pl.when(step == 0)
    def _():
        sums[...] = jnp.zeros_like(sums)

    def run(opened):
        query = q_ref[...]
        cot = cot_ref[0, 0, :BLOCK, :]
        lse, delta = read_stats(cot_ref, width)
        dq = jnp.zeros((width, BLOCK), F32)
        for c in range(opened):
            keys = cut_ref[dev[head, c], 0, :, :width]
            values = cut_ref[dev[head, c], 0, :, width:]
            prob = jnp.exp2(dot(keys, query, NT) * factor - lse)
            dscore = (prob * (dot(values, cot, NT) - delta)).astype(BF16)
            dq = dq + dot(keys, dscore, TN)
            sums[c, :, :width] = sums[c, :, :width] + dot(dscore, query, NN) * scale
            sums[c, :, width:] = sums[c, :, width:] + dot(prob.astype(BF16), cot, NN)
        dq_out[0, 0] = dq

    for opened in range(1, KCUT + 1):
        pl.when(count[head] == opened)(lambda opened=opened: run(opened))

    @pl.when(step == pl.num_programs(1) - 1)
    def _():
        cut_out[0] = sums[...].astype(BF16)


def cut_backward(slot, count, dev, query, cut, cot, heads, width, blocks):
    return pl.pallas_call(
        cut_kernel,
        grid_spec=pltpu.PrefetchScalarGridSpec(
            num_scalar_prefetch=3,
            grid=(heads, blocks),
            in_specs=[
                pl.BlockSpec((BLOCK, width), lambda h, b, s, n, d: (b, h)),
                pl.BlockSpec(
                    (cut.shape[0], 1, BLOCK, 2 * width), lambda h, b, s, n, d: (0, h, 0, 0)
                ),
                pl.BlockSpec(
                    (1, 1, BLOCK + EXTRA, width), lambda h, b, s, n, d: (s[h, b], h, 0, 0)
                ),
            ],
            out_specs=[
                pl.BlockSpec((1, 1, width, BLOCK), lambda h, b, s, n, d: (h, b, 0, 0)),
                pl.BlockSpec((1, KCUT, BLOCK, 2 * width), lambda h, b, s, n, d: (h, 0, 0, 0)),
            ],
            scratch_shapes=[pltpu.VMEM((KCUT, BLOCK, 2 * width), F32)],
        ),
        out_shape=[
            jax.ShapeDtypeStruct((heads, blocks, width, BLOCK), F32),
            jax.ShapeDtypeStruct((heads, KCUT, BLOCK, 2 * width), BF16),
        ],
        compiler_params=params(("arbitrary", "arbitrary")),
        cost_estimate=cost(
            40 * heads * blocks * BLOCK * BLOCK * width, 12 * blocks * BLOCK * heads * width
        ),
        name="cut_backward",
    )(slot, count, dev, query, cut, cot)


def near_kernel(
    slot, peer, which, q_ref, k_ref, v_ref, pair_ref, cot_ref, part_ref, far_q, far_cot,
    dq_out, dk_out, dv_out, keep_out,
):
    width = q_ref.shape[1]
    scale = width ** (-0.5)
    factor = scale * math.log2(math.e)
    keys = k_ref[...]
    values = v_ref[...]

    def terms(k, v, query, cot, stats):
        lse, delta = stats
        prob = jnp.exp2(dot(k, query, NT) * factor - lse)
        dscore = (prob * (dot(v, cot, NT) - delta)).astype(BF16)
        return prob.astype(BF16), dscore

    query = q_ref[...]
    cot = cot_ref[0, 0, :BLOCK, :]
    stats = read_stats(cot_ref, width)
    prob, dscore = terms(keys, values, query, cot, stats)
    dq = part_ref[0, 0] + dot(keys, dscore, TN)
    dk = dot(dscore, query, NN) * scale
    dv = dot(prob, cot, NN)
    pair_keys = pair_ref[0, 0, :, :width]
    _, dscore = terms(pair_keys, pair_ref[0, 0, :, width:], query, cot, stats)
    dq = dq + dot(pair_keys, dscore, TN)
    dq_out[...] = (dq * scale).T.astype(BF16)
    query = far_q[0, 0]
    cot = far_cot[0, 0, :BLOCK, :]
    prob, dscore = terms(keys, values, query, cot, read_stats(far_cot, width))
    dk = dk + (dot(dscore, query, NN) * scale).astype(BF16).astype(F32)
    dv = dv + dot(prob, cot, NN).astype(BF16).astype(F32)
    dk_out[...] = dk.astype(BF16)
    dv_out[...] = dv.astype(BF16)

    @pl.when(which[pl.program_id(0)] == pl.program_id(1))
    def _():
        keep_out[0, :, :width] = dk
        keep_out[0, :, width:] = dv


def near(slot, peer, which, query, keys, values, pair, cot, part, far_q, far_cot, heads, width, blocks):
    rows = pl.BlockSpec((BLOCK, width), lambda h, b, s, p, w: (b, h))
    tall = BLOCK + EXTRA
    return pl.pallas_call(
        near_kernel,
        grid_spec=pltpu.PrefetchScalarGridSpec(
            num_scalar_prefetch=3,
            grid=(heads, blocks),
            in_specs=[
                rows,
                rows,
                rows,
                pl.BlockSpec((1, 1, BLOCK, 2 * width), lambda h, b, s, p, w: (s[h, b], h, 0, 0)),
                pl.BlockSpec((1, 1, tall, width), lambda h, b, s, p, w: (s[h, b], h, 0, 0)),
                pl.BlockSpec((1, 1, width, BLOCK), lambda h, b, s, p, w: (h, b, 0, 0)),
                pl.BlockSpec((1, 1, BLOCK, width), lambda h, b, s, p, w: (p[h, b], h, 0, 0)),
                pl.BlockSpec((1, 1, tall, width), lambda h, b, s, p, w: (p[h, b], h, 0, 0)),
            ],
            out_specs=[
                rows,
                rows,
                rows,
                pl.BlockSpec((1, BLOCK, 2 * width), lambda h, b, s, p, w: (h, 0, 0)),
            ],
        ),
        out_shape=[jax.ShapeDtypeStruct((blocks * BLOCK, heads * width), BF16)] * 3
        + [jax.ShapeDtypeStruct((heads, BLOCK, 2 * width), F32)],
        compiler_params=params(("arbitrary", "arbitrary")),
        cost_estimate=cost(
            50 * heads * blocks * BLOCK * BLOCK * width, 24 * blocks * BLOCK * heads * width
        ),
        name="near",
    )(slot, peer, which, query, keys, values, pair, cot, part, far_q, far_cot)


def patch_kernel(index, term, has, keep_ref, cut_ref, dk_ref, dv_ref, dk_out, dv_out):
    width = dk_ref.shape[1]
    flag = has[pl.program_id(0)] > 0
    total = keep_ref[0] + cut_ref[0, 0].astype(F32)
    dk_out[...] = jnp.where(flag, total[:, :width].astype(BF16), dk_ref[...])
    dv_out[...] = jnp.where(flag, total[:, width:].astype(BF16), dv_ref[...])


def patch(index, term, has, keep, cut, key_grad, value_grad, heads, width):
    rows = pl.BlockSpec((BLOCK, width), lambda h, i, t, f: (i[h], h))
    return pl.pallas_call(
        patch_kernel,
        grid_spec=pltpu.PrefetchScalarGridSpec(
            num_scalar_prefetch=3,
            grid=(heads,),
            in_specs=[
                pl.BlockSpec((1, BLOCK, 2 * width), lambda h, i, t, f: (h, 0, 0)),
                pl.BlockSpec((1, 1, BLOCK, 2 * width), lambda h, i, t, f: (h, t[h], 0, 0)),
                rows,
                rows,
            ],
            out_specs=[rows, rows],
        ),
        out_shape=[jax.ShapeDtypeStruct(key_grad.shape, BF16)] * 2,
        input_output_aliases={5: 0, 6: 1},
        compiler_params=params(("arbitrary",)),
        name="patch",
    )(index, term, has, keep, cut, key_grad, value_grad)


def exchange(x):
    return lax.all_to_all(x, "seq", split_axis=0, concat_axis=0, tiled=True)


def body(query_rows, key_rows, value_rows, out_grad, block_perm, cut_count, norm_gain):
    heads = block_perm.shape[0]
    width = query_rows.shape[1] // heads
    blocks = query_rows.shape[0] // BLOCK
    slots = lax.axis_size("seq")
    features = lax.axis_size("head") * heads * width
    position = lax.axis_index("seq")
    by_dev = block_perm.reshape(heads, slots, blocks)
    local_perm = lax.dynamic_index_in_dim(by_dev, position, 1, keepdims=False)
    recv_slot = local_perm // blocks
    kv_idx = jnp.sum(jnp.where(by_dev // blocks == position, by_dev % blocks, 0), axis=2)
    place = jnp.arange(blocks)
    q_idx = jnp.sum(
        jnp.where(
            recv_slot[:, None, :] == jnp.arange(slots)[None, :, None], place[None, None, :], 0
        ),
        axis=2,
    )
    owned = position * blocks + place
    hits = block_perm[:, None, :] == owned[None, :, None]
    send_slot = jnp.sum(
        jnp.where(hits, (jnp.arange(slots * blocks) // blocks)[None, None, :], 0), axis=2
    )
    cut_global = block_perm[:, :KCUT]
    cut_dev = cut_global // blocks
    cut_mine = cut_dev == position
    cut_has = jnp.sum(cut_mine.astype(jnp.int32), axis=1)
    cut_local = jnp.sum(jnp.where(cut_mine, cut_global % blocks, 0), axis=1)
    cut_term = jnp.sum(jnp.where(cut_mine, jnp.arange(KCUT)[None, :], 0), axis=1)
    gain = norm_gain.reshape(1, heads * width)

    kv_send, q_send, cut_send = pack(
        kv_idx, q_idx, cut_local, key_rows, value_rows, query_rows, slots, heads, width
    )
    cut_rows = lax.all_gather(cut_send, "seq", axis=0, tiled=True)
    kv_recv = exchange(kv_send)
    q_send, kv_recv, cut_rows = lax.optimization_barrier((q_send, kv_recv, cut_rows))
    q_recv = exchange(q_send)
    attn, stat = forward(
        recv_slot, cut_count, cut_dev, query_rows, key_rows, value_rows, kv_recv, cut_rows,
        out_grad, gain, heads, width, blocks,
    )
    sums = lax.psum(jnp.sum(stat[:, :, 1:3, :], axis=0), "head")
    scale_row = lax.rsqrt(sums[:, 0] / features + 1e-06)
    coef = scale_row**3 * sums[:, 1] / features
    row = jnp.stack([scale_row, coef], axis=1)
    normed, cot_send, gain_part = norm(
        recv_slot, attn, out_grad, gain, stat, row, heads, width, blocks, slots
    )
    cot_recv = exchange(cot_send)
    dq_part, cut_part = cut_backward(
        recv_slot, cut_count, cut_dev, query_rows, cut_rows, cot_send, heads, width, blocks
    )
    shares = exchange(cut_part.reshape(slots, heads * KCUT * BLOCK // slots, 2 * width))
    query_grad, key_grad, value_grad, keep = near(
        recv_slot, send_slot, cut_local, query_rows, key_rows, value_rows, kv_recv, cot_send,
        dq_part, q_recv, cot_recv, heads, width, blocks,
    )
    share = jnp.sum(shares.astype(F32), axis=0).astype(BF16)
    depth = share.shape[0]
    tail = jnp.concatenate([share, gain_part.reshape(-1, 2 * width)], axis=0)
    gathered = lax.all_gather(tail, "seq", axis=0)
    cut_total = gathered[:, :depth].reshape(heads, KCUT, BLOCK, 2 * width)
    gain_total = jnp.sum(
        gathered[:, depth:].reshape(slots, heads, EXTRA, width).astype(F32), axis=(0, 2)
    )
    key_grad, value_grad = patch(
        cut_local, cut_term, cut_has, keep, cut_total, key_grad, value_grad, heads, width
    )
    return normed, query_grad, key_grad, value_grad, gain_total.reshape(heads * width)


def solution(mesh):
    rows = P("seq", "head")
    return jax.shard_map(
        body,
        mesh=mesh,
        in_specs=(rows, rows, rows, rows, P("head", None), P("head"), P("head")),
        out_specs=(rows, rows, rows, rows, P("head")),
        check_vma=False,
    )
```

```python
import math

import jax
import jax.numpy as jnp
from jax import lax
from jax.experimental import pallas as pl
from jax.experimental.pallas import tpu as pltpu
from jax.sharding import PartitionSpec as P


BLOCK = 256
KCUT = 4
F32 = jnp.float32
BF16 = jnp.bfloat16
NT = (((1,), (1,)), ((), ()))
TN = (((0,), (0,)), ((), ()))
NN = (((1,), (0,)), ((), ()))
VMEM_LIMIT = 48 * 1024 * 1024


def dot(a, b, dims):
    return lax.dot_general(a, b, dims, preferred_element_type=F32)


def params(semantics):
    return pltpu.CompilerParams(
        dimension_semantics=semantics, vmem_limit_bytes=VMEM_LIMIT
    )


def cost(flops, nbytes):
    return pl.CostEstimate(flops=int(flops), bytes_accessed=int(nbytes), transcendentals=0)


EXTRA = 16


def split3(x):
    first = x.astype(BF16)
    rest = x - first.astype(F32)
    second = rest.astype(BF16)
    third = (rest - second.astype(F32)).astype(BF16)
    return [first.astype(F32), second.astype(F32), third.astype(F32)]


def write_stats(ref, values, width):
    pieces = []
    for value in values:
        for piece in split3(value):
            for start in range(0, BLOCK, width):
                pieces.append(piece[:, start : start + width])
    pieces.append(jnp.zeros((EXTRA - len(pieces), width), F32))
    ref[0, 0, BLOCK:, :] = jnp.concatenate(pieces, axis=0).astype(BF16)


def read_stats(ref, width):
    rows = ref[0, 0, BLOCK:, :].astype(F32)
    halves = BLOCK // width
    values = []
    for v in range(2):
        parts = []
        for h in range(halves):
            base = v * 3 * halves + h
            low = rows[base + 2 * halves : base + 2 * halves + 1]
            mid = rows[base + halves : base + halves + 1]
            parts.append(rows[base : base + 1] + (mid + low))
        values.append(jnp.concatenate(parts, axis=1))
    return values


def pack_kernel(kv_idx, q_idx, c_idx, k_ref, v_ref, q_ref, kc_ref, vc_ref, kv_out, q_out, cut_out):
    width = k_ref.shape[1]
    kv_out[0, 0, :, :width] = k_ref[...]
    kv_out[0, 0, :, width:] = v_ref[...]
    q_out[0, 0] = q_ref[...]

    @pl.when(pl.program_id(1) == 0)
    def _():
        cut_out[0, 0, :, :width] = kc_ref[...]
        cut_out[0, 0, :, width:] = vc_ref[...]


def pack(kv_idx, q_idx, c_idx, keys, values, query, slots, heads, width):
    own = pl.BlockSpec((BLOCK, width), lambda h, s, ki, qi, ci: (ki[h, s], h))
    cut = pl.BlockSpec((BLOCK, width), lambda h, s, ki, qi, ci: (ci[h], h))
    return pl.pallas_call(
        pack_kernel,
        grid_spec=pltpu.PrefetchScalarGridSpec(
            num_scalar_prefetch=3,
            grid=(heads, slots),
            in_specs=[
                own,
                own,
                pl.BlockSpec((BLOCK, width), lambda h, s, ki, qi, ci: (qi[h, s], h)),
                cut,
                cut,
            ],
            out_specs=[
                pl.BlockSpec((1, 1, BLOCK, 2 * width), lambda h, s, ki, qi, ci: (s, h, 0, 0)),
                pl.BlockSpec((1, 1, BLOCK, width), lambda h, s, ki, qi, ci: (s, h, 0, 0)),
                pl.BlockSpec((1, 1, BLOCK, 2 * width), lambda h, s, ki, qi, ci: (0, h, 0, 0)),
            ],
        ),
        out_shape=[
            jax.ShapeDtypeStruct((slots, heads, BLOCK, 2 * width), BF16),
            jax.ShapeDtypeStruct((slots, heads, BLOCK, width), BF16),
            jax.ShapeDtypeStruct((1, heads, BLOCK, 2 * width), BF16),
        ],
        compiler_params=params(("arbitrary", "arbitrary")),
        name="pack",
    )(kv_idx, q_idx, c_idx, keys, values, query, keys, values)


def forward_kernel(
    slot, count, dev, q_ref, k_ref, v_ref, pair_ref, cut_ref, g_ref, gain_ref, attn_out, stat_out, s_buf
):
    head = pl.program_id(0)
    width = q_ref.shape[1]
    factor = width ** (-0.5) * math.log2(math.e)

    def run(opened):
        query = q_ref[...]
        key_list = [k_ref[...], pair_ref[0, 0, :, :width]]
        value_list = [v_ref[...], pair_ref[0, 0, :, width:]]
        for c in range(opened):
            key_list.append(cut_ref[dev[head, c], 0, :, :width])
            value_list.append(cut_ref[dev[head, c], 0, :, width:])
        top = None
        for j, piece in enumerate(key_list):
            s = dot(piece, query, NT)
            s_buf[j] = s
            high = jnp.max(s, axis=0, keepdims=True)
            top = high if top is None else jnp.maximum(top, high)
        top = top * factor
        total = jnp.zeros_like(top)
        acc = jnp.zeros((width, BLOCK), F32)
        for j, piece in enumerate(value_list):
            e = jnp.exp2(s_buf[j] * factor - top)
            total = total + jnp.sum(e, axis=0, keepdims=True)
            acc = acc + dot(piece, e.astype(BF16), TN)
        attn_t = (acc / total).astype(BF16).astype(F32)
        attn_out[...] = attn_t.T.astype(BF16)
        grad_t = (g_ref[...].astype(F32) * gain_ref[...]).T
        lse = top + jnp.log2(total)
        square = jnp.sum(attn_t * attn_t, axis=0, keepdims=True)
        mix = jnp.sum(grad_t * attn_t, axis=0, keepdims=True)
        stat_out[0, 0] = jnp.concatenate(
            [lse, square, mix, jnp.zeros((5, BLOCK), F32)], axis=0
        )

    for opened in range(1, KCUT + 1):
        pl.when(count[head] == opened)(lambda opened=opened: run(opened))


def forward(slot, count, dev, query, keys, values, pair, cut, grad, gain, heads, width, blocks):
    rows = pl.BlockSpec((BLOCK, width), lambda h, b, s, n, d: (b, h))
    return pl.pallas_call(
        forward_kernel,
        grid_spec=pltpu.PrefetchScalarGridSpec(
            num_scalar_prefetch=3,
            grid=(heads, blocks),
            in_specs=[
                rows,
                rows,
                rows,
                pl.BlockSpec((1, 1, BLOCK, 2 * width), lambda h, b, s, n, d: (s[h, b], h, 0, 0)),
                pl.BlockSpec((cut.shape[0], 1, BLOCK, 2 * width), lambda h, b, s, n, d: (0, h, 0, 0)),
                rows,
                pl.BlockSpec((1, width), lambda h, b, s, n, d: (0, h)),
            ],
            out_specs=[
                rows,
                pl.BlockSpec((1, 1, 8, BLOCK), lambda h, b, s, n, d: (h, b, 0, 0)),
            ],
            scratch_shapes=[pltpu.VMEM((2 + KCUT, BLOCK, BLOCK), F32)],
        ),
        out_shape=[
            jax.ShapeDtypeStruct((blocks * BLOCK, heads * width), BF16),
            jax.ShapeDtypeStruct((heads, blocks, 8, BLOCK), F32),
        ],
        compiler_params=params(("arbitrary", "arbitrary")),
        cost_estimate=cost(
            4 * heads * blocks * BLOCK * BLOCK * 6 * width, 10 * blocks * BLOCK * heads * width
        ),
        name="forward",
    )(slot, count, dev, query, keys, values, pair, cut, grad, gain)


def norm_kernel(
    slot, attn_ref, g_ref, gain_ref, stat_ref, row_ref, norm_out, cot_out, gain_out, gain_buf
):
    width = attn_ref.shape[1]
    attn = attn_ref[...].astype(F32)
    grad = g_ref[...].astype(F32)
    gain = gain_ref[...]
    scale = jnp.broadcast_to(row_ref[0, 0:1, :], (width, BLOCK)).T
    coef = jnp.broadcast_to(row_ref[0, 1:2, :], (width, BLOCK)).T
    scaled = attn * scale
    norm_out[...] = (scaled * gain).astype(BF16)
    cot = (scale * gain * grad - attn * coef).astype(BF16)
    cot_out[0, 0, :BLOCK, :] = cot
    delta = jnp.sum((cot.astype(F32) * attn).T, axis=0, keepdims=True)
    write_stats(cot_out, [stat_ref[0, 0, 0:1, :], delta], width)
    part = jnp.sum((grad * scaled).reshape(BLOCK // 8, 8, width), axis=0)

    @pl.when(pl.program_id(1) == 0)
    def _():
        gain_buf[...] = part

    @pl.when(pl.program_id(1) > 0)
    def _():
        gain_buf[...] = gain_buf[...] + part

    @pl.when(pl.program_id(1) == pl.num_programs(1) - 1)
    def _():
        pieces = split3(jnp.sum(gain_buf[...], axis=0, keepdims=True))
        pieces.append(jnp.zeros((EXTRA - 3, width), F32))
        gain_out[0] = jnp.concatenate(pieces, axis=0).astype(BF16)


def norm(slot, attn, grad, gain, stat, row, heads, width, blocks, slots):
    rows = pl.BlockSpec((BLOCK, width), lambda h, b, s: (b, h))
    return pl.pallas_call(
        norm_kernel,
        grid_spec=pltpu.PrefetchScalarGridSpec(
            num_scalar_prefetch=1,
            grid=(heads, blocks),
            in_specs=[
                rows,
                rows,
                pl.BlockSpec((1, width), lambda h, b, s: (0, h)),
                pl.BlockSpec((1, 1, 8, BLOCK), lambda h, b, s: (h, b, 0, 0)),
                pl.BlockSpec((1, 2, BLOCK), lambda h, b, s: (b, 0, 0)),
            ],
            out_specs=[
                rows,
                pl.BlockSpec((1, 1, BLOCK + EXTRA, width), lambda h, b, s: (s[h, b], h, 0, 0)),
                pl.BlockSpec((1, EXTRA, width), lambda h, b, s: (h, 0, 0)),
            ],
            scratch_shapes=[pltpu.VMEM((8, width), F32)],
        ),
        out_shape=[
            jax.ShapeDtypeStruct((blocks * BLOCK, heads * width), BF16),
            jax.ShapeDtypeStruct((slots, heads, BLOCK + EXTRA, width), BF16),
            jax.ShapeDtypeStruct((heads, EXTRA, width), BF16),
        ],
        compiler_params=params(("arbitrary", "arbitrary")),
        name="norm",
    )(slot, attn, grad, gain, stat, row)


def cut_kernel(slot, count, dev, q_ref, cut_ref, cot_ref, dq_out, cut_out, sums):
    head = pl.program_id(0)
    step = pl.program_id(1)
    width = q_ref.shape[1]
    scale = width ** (-0.5)
    factor = scale * math.log2(math.e)

    @pl.when(step == 0)
    def _():
        sums[...] = jnp.zeros_like(sums)

    def run(opened):
        query = q_ref[...]
        cot = cot_ref[0, 0, :BLOCK, :]
        lse, delta = read_stats(cot_ref, width)
        dq = jnp.zeros((width, BLOCK), F32)
        for c in range(opened):
            keys = cut_ref[dev[head, c], 0, :, :width]
            values = cut_ref[dev[head, c], 0, :, width:]
            prob = jnp.exp2(dot(keys, query, NT) * factor - lse)
            dscore = (prob * (dot(values, cot, NT) - delta)).astype(BF16)
            dq = dq + dot(keys, dscore, TN)
            sums[c, :, :width] = sums[c, :, :width] + dot(dscore, query, NN) * scale
            sums[c, :, width:] = sums[c, :, width:] + dot(prob.astype(BF16), cot, NN)
        dq_out[0, 0] = dq

    for opened in range(1, KCUT + 1):
        pl.when(count[head] == opened)(lambda opened=opened: run(opened))

    @pl.when(step == pl.num_programs(1) - 1)
    def _():
        cut_out[0] = sums[...].astype(BF16)


def cut_backward(slot, count, dev, query, cut, cot, heads, width, blocks):
    return pl.pallas_call(
        cut_kernel,
        grid_spec=pltpu.PrefetchScalarGridSpec(
            num_scalar_prefetch=3,
            grid=(heads, blocks),
            in_specs=[
                pl.BlockSpec((BLOCK, width), lambda h, b, s, n, d: (b, h)),
                pl.BlockSpec(
                    (cut.shape[0], 1, BLOCK, 2 * width), lambda h, b, s, n, d: (0, h, 0, 0)
                ),
                pl.BlockSpec(
                    (1, 1, BLOCK + EXTRA, width), lambda h, b, s, n, d: (s[h, b], h, 0, 0)
                ),
            ],
            out_specs=[
                pl.BlockSpec((1, 1, width, BLOCK), lambda h, b, s, n, d: (h, b, 0, 0)),
                pl.BlockSpec((1, KCUT, BLOCK, 2 * width), lambda h, b, s, n, d: (h, 0, 0, 0)),
            ],
            scratch_shapes=[pltpu.VMEM((KCUT, BLOCK, 2 * width), F32)],
        ),
        out_shape=[
            jax.ShapeDtypeStruct((heads, blocks, width, BLOCK), F32),
            jax.ShapeDtypeStruct((heads, KCUT, BLOCK, 2 * width), BF16),
        ],
        compiler_params=params(("arbitrary", "arbitrary")),
        cost_estimate=cost(
            40 * heads * blocks * BLOCK * BLOCK * width, 12 * blocks * BLOCK * heads * width
        ),
        name="cut_backward",
    )(slot, count, dev, query, cut, cot)


def near_kernel(
    slot, peer, which, q_ref, k_ref, v_ref, pair_ref, cot_ref, part_ref, far_q, far_cot,
    dq_out, dk_out, dv_out, keep_out,
):
    width = q_ref.shape[1]
    scale = width ** (-0.5)
    factor = scale * math.log2(math.e)
    keys = k_ref[...]
    values = v_ref[...]

    def terms(k, v, query, cot, stats):
        lse, delta = stats
        prob = jnp.exp2(dot(k, query, NT) * factor - lse)
        dscore = (prob * (dot(v, cot, NT) - delta)).astype(BF16)
        return prob.astype(BF16), dscore

    query = q_ref[...]
    cot = cot_ref[0, 0, :BLOCK, :]
    stats = read_stats(cot_ref, width)
    prob, dscore = terms(keys, values, query, cot, stats)
    dq = part_ref[0, 0] + dot(keys, dscore, TN)
    dk = dot(dscore, query, NN) * scale
    dv = dot(prob, cot, NN)
    pair_keys = pair_ref[0, 0, :, :width]
    _, dscore = terms(pair_keys, pair_ref[0, 0, :, width:], query, cot, stats)
    dq = dq + dot(pair_keys, dscore, TN)
    dq_out[...] = (dq * scale).T.astype(BF16)
    query = far_q[0, 0]
    cot = far_cot[0, 0, :BLOCK, :]
    prob, dscore = terms(keys, values, query, cot, read_stats(far_cot, width))
    dk = dk + (dot(dscore, query, NN) * scale).astype(BF16).astype(F32)
    dv = dv + dot(prob, cot, NN).astype(BF16).astype(F32)
    dk_out[...] = dk.astype(BF16)
    dv_out[...] = dv.astype(BF16)

    @pl.when(which[pl.program_id(0)] == pl.program_id(1))
    def _():
        keep_out[0, :, :width] = dk
        keep_out[0, :, width:] = dv


def near(slot, peer, which, query, keys, values, pair, cot, part, far_q, far_cot, heads, width, blocks):
    rows = pl.BlockSpec((BLOCK, width), lambda h, b, s, p, w: (b, h))
    tall = BLOCK + EXTRA
    return pl.pallas_call(
        near_kernel,
        grid_spec=pltpu.PrefetchScalarGridSpec(
            num_scalar_prefetch=3,
            grid=(heads, blocks),
            in_specs=[
                rows,
                rows,
                rows,
                pl.BlockSpec((1, 1, BLOCK, 2 * width), lambda h, b, s, p, w: (s[h, b], h, 0, 0)),
                pl.BlockSpec((1, 1, tall, width), lambda h, b, s, p, w: (s[h, b], h, 0, 0)),
                pl.BlockSpec((1, 1, width, BLOCK), lambda h, b, s, p, w: (h, b, 0, 0)),
                pl.BlockSpec((1, 1, BLOCK, width), lambda h, b, s, p, w: (p[h, b], h, 0, 0)),
                pl.BlockSpec((1, 1, tall, width), lambda h, b, s, p, w: (p[h, b], h, 0, 0)),
            ],
            out_specs=[
                rows,
                rows,
                rows,
                pl.BlockSpec((1, BLOCK, 2 * width), lambda h, b, s, p, w: (h, 0, 0)),
            ],
        ),
        out_shape=[jax.ShapeDtypeStruct((blocks * BLOCK, heads * width), BF16)] * 3
        + [jax.ShapeDtypeStruct((heads, BLOCK, 2 * width), F32)],
        compiler_params=params(("arbitrary", "arbitrary")),
        cost_estimate=cost(
            50 * heads * blocks * BLOCK * BLOCK * width, 24 * blocks * BLOCK * heads * width
        ),
        name="near",
    )(slot, peer, which, query, keys, values, pair, cot, part, far_q, far_cot)


def patch_kernel(index, term, has, keep_ref, cut_ref, dk_ref, dv_ref, dk_out, dv_out):
    width = dk_ref.shape[1]
    flag = has[pl.program_id(0)] > 0
    total = keep_ref[0] + cut_ref[0, 0].astype(F32)
    dk_out[...] = jnp.where(flag, total[:, :width].astype(BF16), dk_ref[...])
    dv_out[...] = jnp.where(flag, total[:, width:].astype(BF16), dv_ref[...])


def patch(index, term, has, keep, cut, key_grad, value_grad, heads, width):
    rows = pl.BlockSpec((BLOCK, width), lambda h, i, t, f: (i[h], h))
    return pl.pallas_call(
        patch_kernel,
        grid_spec=pltpu.PrefetchScalarGridSpec(
            num_scalar_prefetch=3,
            grid=(heads,),
            in_specs=[
                pl.BlockSpec((1, BLOCK, 2 * width), lambda h, i, t, f: (h, 0, 0)),
                pl.BlockSpec((1, 1, BLOCK, 2 * width), lambda h, i, t, f: (h, t[h], 0, 0)),
                rows,
                rows,
            ],
            out_specs=[rows, rows],
        ),
        out_shape=[jax.ShapeDtypeStruct(key_grad.shape, BF16)] * 2,
        input_output_aliases={5: 0, 6: 1},
        compiler_params=params(("arbitrary",)),
        name="patch",
    )(index, term, has, keep, cut, key_grad, value_grad)


def exchange_slots(x):
    return lax.all_to_all(x, "seq", split_axis=0, concat_axis=0, tiled=True)


def body(query_rows, key_rows, value_rows, out_grad, block_perm, cut_count, norm_gain):
    heads = block_perm.shape[0]
    width = query_rows.shape[1] // heads
    blocks = query_rows.shape[0] // BLOCK
    slots = lax.axis_size("seq")
    features = lax.axis_size("head") * heads * width
    position = lax.axis_index("seq")
    by_dev = block_perm.reshape(heads, slots, blocks)
    local_perm = lax.dynamic_index_in_dim(by_dev, position, 1, keepdims=False)
    recv_slot = local_perm // blocks
    kv_idx = jnp.sum(jnp.where(by_dev // blocks == position, by_dev % blocks, 0), axis=2)
    place = jnp.arange(blocks)
    q_idx = jnp.sum(
        jnp.where(
            recv_slot[:, None, :] == jnp.arange(slots)[None, :, None], place[None, None, :], 0
        ),
        axis=2,
    )
    owned = position * blocks + place
    hits = block_perm[:, None, :] == owned[None, :, None]
    send_slot = jnp.sum(
        jnp.where(hits, (jnp.arange(slots * blocks) // blocks)[None, None, :], 0), axis=2
    )
    cut_global = block_perm[:, :KCUT]
    cut_dev = cut_global // blocks
    cut_mine = cut_dev == position
    cut_has = jnp.sum(cut_mine.astype(jnp.int32), axis=1)
    cut_local = jnp.sum(jnp.where(cut_mine, cut_global % blocks, 0), axis=1)
    cut_term = jnp.sum(jnp.where(cut_mine, jnp.arange(KCUT)[None, :], 0), axis=1)
    gain = norm_gain.reshape(1, heads * width)

    kv_send, q_send, cut_send = pack(
        kv_idx, q_idx, cut_local, key_rows, value_rows, query_rows, slots, heads, width
    )
    cut_rows = lax.all_gather(cut_send, "seq", axis=0, tiled=True)
    kv_recv = exchange_slots(kv_send)
    q_send, kv_recv, cut_rows = lax.optimization_barrier((q_send, kv_recv, cut_rows))
    q_recv = exchange_slots(q_send)
    attn, stat = forward(
        recv_slot, cut_count, cut_dev, query_rows, key_rows, value_rows, kv_recv, cut_rows,
        out_grad, gain, heads, width, blocks,
    )
    sums = lax.psum(jnp.sum(stat[:, :, 1:3, :], axis=0), "head")
    scale_row = lax.rsqrt(sums[:, 0] / features + 1e-06)
    coef = scale_row**3 * sums[:, 1] / features
    row = jnp.stack([scale_row, coef], axis=1)
    normed, cot_send, gain_part = norm(
        recv_slot, attn, out_grad, gain, stat, row, heads, width, blocks, slots
    )
    cot_recv = exchange_slots(cot_send)
    dq_part, cut_part = cut_backward(
        recv_slot, cut_count, cut_dev, query_rows, cut_rows, cot_send, heads, width, blocks
    )
    shares = exchange_slots(cut_part.reshape(slots, heads * KCUT * BLOCK // slots, 2 * width))
    query_grad, key_grad, value_grad, keep = near(
        recv_slot, send_slot, cut_local, query_rows, key_rows, value_rows, kv_recv, cot_send,
        dq_part, q_recv, cot_recv, heads, width, blocks,
    )
    share = jnp.sum(shares.astype(F32), axis=0).astype(BF16)
    depth = share.shape[0]
    tail = jnp.concatenate([share, gain_part.reshape(-1, 2 * width)], axis=0)
    gathered = lax.all_gather(tail, "seq", axis=0)
    cut_total = gathered[:, :depth].reshape(heads, KCUT, BLOCK, 2 * width)
    gain_total = jnp.sum(
        gathered[:, depth:].reshape(slots, heads, EXTRA, width).astype(F32), axis=(0, 2)
    )
    key_grad, value_grad = patch(
        cut_local, cut_term, cut_has, keep, cut_total, key_grad, value_grad, heads, width
    )
    return normed, query_grad, key_grad, value_grad, gain_total.reshape(heads * width)


def solution(mesh):
    rows = P("seq", "head")
    return jax.shard_map(
        body,
        mesh=mesh,
        in_specs=(rows, rows, rows, rows, P("head", None), P("head"), P("head")),
        out_specs=(rows, rows, rows, rows, P("head")),
        check_vma=False,
    )
```
